32 devices in a mesh: seq: 8 (over y, x, core), head: 4 (over z).
Axes of the slice: x: 2, y: 2, z: 4, core: 2. Of those that a mesh axis runs over, the one named last changes fastest.
Arguments:
- queries: bfloat16 [6144, 2048], P('seq', 'head'), may hold values from -6 to 6
- keys: bfloat16 [6144, 2048], P('seq', 'head'), may hold values from -6 to 6
- values: bfloat16 [6144, 2048], P('seq', 'head'), may hold values from -6 to 6
- out_weight: bfloat16 [2048, 6144], P('head'), may hold values from -0.1875 to 0.1875
- cotangent: bfloat16 [6144, 6144], P('seq', 'head'), may hold values from -6 to 6
Outputs:
- mixed: bfloat16 [6144, 6144], P('seq', 'head')
- query_grad: bfloat16 [6144, 2048], P('seq', 'head')
- key_grad: bfloat16 [6144, 2048], P('seq', 'head')
- value_grad: bfloat16 [6144, 2048], P('seq', 'head')
The draws below stay inside these ranges and needn't reach their ends.
All inputs are finite; a program needn't handle non-finite values.
Results may differ from the reference program's by a relative error of at most 0.019.
Values may be sent and summed in bfloat16 or wider, within the bound.
No kernel may reach another device: no remote copies, remote signals or barrier semaphores. Data moves between devices by JAX's collectives and lax.ppermute only.
A program may use at most 128 MiB of HBM per device.

```python
import jax
import jax.numpy as jnp
from jax import lax

D = 6144
HEAD_DIM = 128
HEADS_DEV = 4
TOK_DEV = 768
HEADS = 16
TOKENS = 6144
N_SEQ = 8
N_HEAD = 4


def spiked(result, rng, source, target, shards_of, factor):
    owner, partner = [(jnp.arange(result.shape[axis_at]) // (result.shape[axis_at] // shards_of)).reshape([-1 if axis == axis_at else 1 for axis in range(result.ndim)]) for axis_at in (source, target)]
    chosen = jax.random.permutation(rng, shards_of)[partner]
    strong = (owner == chosen) | (owner == (partner + shards_of // 2) % shards_of)
    return jnp.where(strong, factor * result, result)


def block_levels(rng, extent, shards, low, top_value):
    level = 1.0
    for axis_at, blocks in shards:
        heights = jax.random.uniform(jax.random.fold_in(jax.random.fold_in(rng, 6), axis_at), (blocks,), jnp.float32, low / len(shards), top_value / len(shards))
        level = level * jnp.repeat(jnp.exp(heights), extent[axis_at] // blocks).reshape((-1,) + (1,) * (len(extent) - 1 - axis_at))
    return level


def bell_draw(key, shape, scale, reach, cuts=(), kind=jnp.bfloat16):
    loudness = block_levels(key, shape, cuts, -0.22, 0.18) if cuts else 1.0
    values = jax.random.normal(key, shape, jnp.float32) * scale * loudness
    return jnp.minimum(jnp.maximum(values, -reach), reach).astype(kind)


def heavy_noise(rng, dims, spread, reach, pieces, heavy, dtype=jnp.bfloat16):
    drawn = spread * jax.random.normal(rng, dims, jnp.float32)
    if pieces:
        drawn = drawn * block_levels(rng, dims, pieces, -0.22, 0.18)
    return jnp.clip(spiked(drawn, jax.random.fold_in(rng, 3), *heavy), -reach, reach).astype(dtype)


def setup_inputs(seed: int = 0) -> dict:
    splits = jax.random.split(jax.random.key(seed), 6)
    queries = bell_draw(splits[0], (TOKENS, HEADS * HEAD_DIM), 1.0, 6.0, ((0, 8), (1, 4)))
    keys = bell_draw(splits[1], (TOKENS, HEADS * HEAD_DIM), 1.0, 6.0, ((0, 8), (1, 4)))
    values = bell_draw(splits[2], (TOKENS, HEADS * HEAD_DIM), 1.0, 6.0, ((0, 8), (1, 4)))
    out_weight = heavy_noise(splits[3], (HEADS * HEAD_DIM, D), (HEADS * HEAD_DIM) ** -0.5, 0.1875, ((0, 4),), (0, 1, 4, 2.0))
    cotangent = bell_draw(splits[4], (TOKENS, D), 1.0, 6.0, ((0, 8), (1, 4)))
    return dict(queries=queries, keys=keys, values=values, out_weight=out_weight, cotangent=cotangent)


epsilon = 1e-06

def causal_mask(length):
    rows = lax.broadcasted_iota(jnp.int32, (length, length), 0)
    cols = lax.broadcasted_iota(jnp.int32, (length, length), 1)
    return rows >= cols

def forward_block(running, block):
    query_heads, key_heads, value_heads = block
    qf = query_heads.astype(jnp.float32)
    kf = key_heads.astype(jnp.float32)
    vf = value_heads.astype(jnp.float32)
    causal = causal_mask(qf.shape[0])
    scored = jnp.einsum('thd,shd->hts', qf, kf)
    mixing = jnp.where(causal[None], scored, 0.0).astype(jnp.bfloat16)
    inner_part = jnp.einsum('hts,shd->thd', mixing.astype(jnp.float32), vf)
    outer_part = jnp.einsum('thi,hij->thj', qf, running, precision=lax.Precision.HIGHEST)
    head_out = inner_part + outer_part
    inverse = lax.rsqrt(lax.optimization_barrier(jnp.mean(head_out * head_out, axis=-1, keepdims=True)) + epsilon)
    normed = head_out * inverse
    updated = running + jnp.einsum('thi,thj->hij', kf, vf)
    return (updated, (normed, inverse, running, mixing))

def backward_block(running, block):
    query_heads, key_heads, value_heads, grad_heads, mixing, state = block
    qf = query_heads.astype(jnp.float32)
    kf = key_heads.astype(jnp.float32)
    vf = value_heads.astype(jnp.float32)
    gf = grad_heads.astype(jnp.float32)
    causal = causal_mask(qf.shape[0])
    cross = jnp.where(causal[None], jnp.einsum('thd,shd->hts', gf, vf), 0.0).astype(jnp.bfloat16)
    crossf = cross.astype(jnp.float32)
    mixf = mixing.astype(jnp.float32)
    high = lax.Precision.HIGHEST
    query_grad = jnp.einsum('hts,shd->thd', crossf, kf) + jnp.einsum('thj,hij->thi', gf, state, precision=high)
    key_grad = jnp.einsum('hts,thd->shd', crossf, qf) + jnp.einsum('shj,hij->shi', vf, running, precision=high)
    value_grad = jnp.einsum('hts,thd->shd', mixf, gf) + jnp.einsum('shi,hij->shj', kf, running, precision=high)
    updated = running + jnp.einsum('thi,thj->hij', qf, gf)
    return (updated, (query_grad.astype(jnp.bfloat16), key_grad.astype(jnp.bfloat16), value_grad.astype(jnp.bfloat16)))

def reference(queries, keys, values, out_weight, cotangent):
    shape_blocks = (N_SEQ, TOK_DEV, HEADS, HEAD_DIM)
    query_blocks = queries.reshape(shape_blocks)
    key_blocks = keys.reshape(shape_blocks)
    value_blocks = values.reshape(shape_blocks)
    start_state = jnp.zeros((HEADS, HEAD_DIM, HEAD_DIM), jnp.float32)
    unused, saved = lax.scan(forward_block, start_state, (query_blocks, key_blocks, value_blocks))
    normed, inverse, states, mixings = saved
    flat_normed = normed.reshape(TOKENS, HEADS * HEAD_DIM).astype(jnp.bfloat16)
    group_width = HEADS_DEV * HEAD_DIM
    total = jnp.zeros((TOKENS, D), jnp.float32)
    for group in range(N_HEAD):
        lower = group * group_width
        partial_out = jnp.dot(flat_normed[:, lower:lower + group_width], out_weight[lower:lower + group_width], preferred_element_type=jnp.float32)
        total = total + lax.optimization_barrier(partial_out.astype(jnp.bfloat16)).astype(jnp.float32)
    mixed = total.astype(jnp.bfloat16)
    grad_normed = jnp.dot(cotangent, out_weight.T, preferred_element_type=jnp.float32).reshape(shape_blocks)
    aligned = lax.optimization_barrier(jnp.mean(grad_normed * normed, axis=-1, keepdims=True))
    grad_heads = (inverse * (grad_normed - normed * aligned)).astype(jnp.bfloat16)
    unused_two, grads = lax.scan(backward_block, start_state, (query_blocks, key_blocks, value_blocks, grad_heads, mixings, states), reverse=True)
    query_grad, key_grad, value_grad = grads
    flat = (TOKENS, HEADS * HEAD_DIM)
    return (mixed, query_grad.reshape(flat), key_grad.reshape(flat), value_grad.reshape(flat))
```

```python
import functools

import jax
import jax.numpy as jnp
from jax import lax
from jax.experimental import pallas as pl
from jax.experimental.pallas import tpu as pltpu
from jax.sharding import PartitionSpec as P

HEAD_DIM = 128
EPSILON = 1e-06
F32 = jnp.float32
BF16 = jnp.bfloat16


def dot(a, b, dims):
    return lax.dot_general(a, b, ((dims[:1], dims[1:]), ((), ())), preferred_element_type=F32)


def mm(a, b):
    return dot(a, b, (1, 0))


def mmt(a, b):
    return dot(a, b, (1, 1))


def tmm(a, b):
    return dot(a, b, (0, 0))


def block_of(extent, most):
    for size in (most, most // 2, most // 4):
        if extent % size == 0:
            return size
    return extent


def head_spec(tokens):
    return pl.BlockSpec((tokens, HEAD_DIM), lambda h: (0, h))


SQUARE = pl.BlockSpec((1, HEAD_DIM, HEAD_DIM), lambda h: (h, 0, 0))


def cost(flops, nbytes):
    return pl.CostEstimate(flops=int(flops), bytes_accessed=int(nbytes), transcendentals=0)


def later_key(rows, cols, base):
    at = lax.broadcasted_iota(jnp.int32, (rows, cols), 0) + base
    return at >= lax.broadcasted_iota(jnp.int32, (rows, cols), 1)


def later_query(rows, cols):
    at = lax.broadcasted_iota(jnp.int32, (rows, cols), 0)
    return lax.broadcasted_iota(jnp.int32, (rows, cols), 1) >= at


def outer_kernel(a_ref, b_ref, out_ref):
    out_ref[0] = tmm(a_ref[...], b_ref[...])


def outer(a, b):
    tokens, width = a.shape
    heads = width // HEAD_DIM
    return pl.pallas_call(
        outer_kernel,
        out_shape=jax.ShapeDtypeStruct((heads, HEAD_DIM, HEAD_DIM), F32),
        grid=(heads,),
        in_specs=[head_spec(tokens)] * 2,
        out_specs=SQUARE,
        cost_estimate=cost(2 * tokens * width * HEAD_DIM, 4 * tokens * width),
        name="outer",
    )(a, b)


def forward_kernel(step, q_ref, k_ref, v_ref, state_ref, out_ref, normed_ref):
    tokens = q_ref.shape[0]
    state = state_ref[0].astype(BF16)
    for first in range(0, tokens, step):
        last = first + step
        q = q_ref[first:last, :]
        mixing = mmt(q, k_ref[:last, :])
        mixing = jnp.where(later_key(step, last, first), mixing, 0.0).astype(BF16)
        out = mm(mixing, v_ref[:last, :]) + mm(q, state)
        inverse = lax.rsqrt(jnp.mean(out * out, axis=-1, keepdims=True) + EPSILON)
        out_ref[first:last, :] = out
        normed_ref[first:last, :] = (out * inverse).astype(BF16)


def forward(q, k, v, state):
    tokens, width = q.shape
    spec = head_spec(tokens)
    return pl.pallas_call(
        functools.partial(forward_kernel, block_of(tokens, 256)),
        out_shape=(jax.ShapeDtypeStruct(q.shape, F32), jax.ShapeDtypeStruct(q.shape, BF16)),
        grid=(width // HEAD_DIM,),
        in_specs=[spec] * 3 + [SQUARE],
        out_specs=(spec, spec),
        cost_estimate=cost(4 * tokens * tokens * width, 12 * tokens * width),
        name="forward",
    )(q, k, v, state)


def place(piece_refs, starts, weight_ref):
    for ref, start in zip(piece_refs, starts):
        rows = ref.shape[0]
        weight_ref[pl.ds(pl.multiple_of(start * rows, rows), rows), :] = ref[...]


def partial_kernel(order, where_ref, cot_ref, *refs):
    pieces, (out_ref, weight_ref, total_ref) = refs[: len(order)], refs[len(order) :]
    at = pl.program_id(0)
    place(pieces, [where_ref[0] ^ m for m in order], weight_ref)
    part = mmt(cot_ref[...], weight_ref[...])

    @pl.when(at == 0)
    def _():
        total_ref[...] = part

    @pl.when(at > 0)
    def _():
        total_ref[...] += part

    @pl.when(at == pl.num_programs(0) - 1)
    def _():
        out_ref[...] = total_ref[...].astype(out_ref.dtype)


def partial(where, cot, pieces, order, rows):
    tokens, depth = cot.shape
    step = block_of(depth, 512)
    return pl.pallas_call(
        functools.partial(partial_kernel, order),
        out_shape=jax.ShapeDtypeStruct((tokens, rows), BF16),
        grid_spec=pltpu.PrefetchScalarGridSpec(
            num_scalar_prefetch=1,
            grid=(depth // step,),
            in_specs=[pl.BlockSpec((tokens, step), lambda i, w: (0, i))]
            + [pl.BlockSpec((p.shape[0], step), lambda i, w: (0, i)) for p in pieces],
            out_specs=pl.BlockSpec((tokens, rows), lambda i, w: (0, 0)),
            scratch_shapes=[pltpu.VMEM((rows, step), BF16), pltpu.VMEM((tokens, rows), F32)],
        ),
        cost_estimate=cost(2 * tokens * depth * rows, 2 * (tokens + rows) * depth),
        name="partial",
    )(where, cot, *pieces)


def own_partial_kernel(where_ref, cot_ref, weight_ref, out_ref):
    part = mmt(cot_ref[...], weight_ref[...])

    @pl.when(pl.program_id(0) == 0)
    def _():
        out_ref[...] = part

    @pl.when(pl.program_id(0) > 0)
    def _():
        out_ref[...] += part


def own_partial(where, cot, weight):
    tokens, depth = cot.shape
    rows = weight.shape[0]
    step = block_of(depth, 512)
    count = depth // step
    return pl.pallas_call(
        own_partial_kernel,
        out_shape=jax.ShapeDtypeStruct((tokens, rows), F32),
        grid_spec=pltpu.PrefetchScalarGridSpec(
            num_scalar_prefetch=1,
            grid=(count,),
            in_specs=[
                pl.BlockSpec((tokens, step), lambda i, w: (0, i)),
                pl.BlockSpec((rows, step), lambda i, w: (0, w[1] * count + i)),
            ],
            out_specs=pl.BlockSpec((tokens, rows), lambda i, w: (0, 0)),
        ),
        cost_estimate=cost(2 * tokens * depth * rows, 2 * (tokens + rows) * depth),
        name="own_partial",
    )(where, cot, weight)


def mixed_kernel(counts, order, where_ref, own_ref, weight_ref, *refs):
    refs = list(refs)
    total = mm(own_ref[...], weight_ref[...])
    out_ref, scratch_ref = refs[-2], refs[-1]
    for normed_count in counts:
        normed = refs.pop(0)[...]
        for _ in range(normed_count - 1):
            normed = normed + refs.pop(0)[...]
        pieces = [refs.pop(0) for _ in order]
        place(pieces, [where_ref[0] ^ m for m in order], scratch_ref)
        total += mm(normed, scratch_ref[...])
    out_ref[...] = total.astype(BF16)


def mix(where, own, weight, groups, order, columns):
    tokens, rows = own.shape
    step = block_of(columns, 512)
    count = columns // step
    full = pl.BlockSpec((tokens, rows), lambda i, w: (0, 0))
    specs, operands = [full, pl.BlockSpec((rows, step), lambda i, w: (0, w[1] * count + i))], [own, weight]
    for normeds, pieces in groups:
        specs += [full] * len(normeds)
        specs += [pl.BlockSpec((p.shape[0], step), lambda i, w: (0, i)) for p in pieces]
        operands += [*normeds, *pieces]
    n = len(groups) + 1
    return pl.pallas_call(
        functools.partial(mixed_kernel, [len(g[0]) for g in groups], order),
        out_shape=jax.ShapeDtypeStruct((tokens, columns), BF16),
        grid_spec=pltpu.PrefetchScalarGridSpec(
            num_scalar_prefetch=1,
            grid=(count,),
            in_specs=specs,
            out_specs=pl.BlockSpec((tokens, step), lambda i, w: (0, i)),
            scratch_shapes=[pltpu.VMEM((rows, step), BF16)],
        ),
        cost_estimate=cost(2 * tokens * rows * n * columns, 2 * n * rows * (tokens + columns)),
        name="mix",
    )(where, *operands)


def grad_heads_kernel(own_ref, up_ref, down_ref, out_ref, q_ref, grad_ref, local_ref):
    grad = own_ref[...] + up_ref[...].astype(F32) + down_ref[...].astype(F32)
    out = out_ref[...]
    inverse = lax.rsqrt(jnp.mean(out * out, axis=-1, keepdims=True) + EPSILON)
    normed = out * inverse
    aligned = jnp.mean(grad * normed, axis=-1, keepdims=True)
    grad = (inverse * (grad - normed * aligned)).astype(BF16)
    grad_ref[...] = grad
    local_ref[0] = tmm(q_ref[...], grad)


def grad_heads(own, up, down, out, q):
    tokens, width = q.shape
    heads = width // HEAD_DIM
    spec = head_spec(tokens)
    return pl.pallas_call(
        grad_heads_kernel,
        out_shape=(
            jax.ShapeDtypeStruct(q.shape, BF16),
            jax.ShapeDtypeStruct((heads, HEAD_DIM, HEAD_DIM), F32),
        ),
        grid=(heads,),
        in_specs=[spec] * 5,
        out_specs=(spec, SQUARE),
        cost_estimate=cost(2 * tokens * width * HEAD_DIM, 16 * tokens * width),
        name="grad_heads",
    )(own, up, down, out, q)


def inner_kernel(step, q_ref, k_ref, v_ref, grad_ref, state_ref, qg_ref, kp_ref, vp_ref):
    tokens = q_ref.shape[0]
    state = state_ref[0].astype(BF16)
    for first in range(0, tokens, step):
        last = first + step
        grad = grad_ref[first:last, :]
        cross = mmt(grad, v_ref[:last, :])
        cross = jnp.where(later_key(step, last, first), cross, 0.0).astype(BF16)
        qg_ref[first:last, :] = (mm(cross, k_ref[:last, :]) + mmt(grad, state)).astype(BF16)
        keep = later_query(step, tokens - first)
        cross = mmt(v_ref[first:last, :], grad_ref[first:, :])
        cross = jnp.where(keep, cross, 0.0).astype(BF16)
        kp_ref[first:last, :] = mm(cross, q_ref[first:, :])
        mixing = mmt(k_ref[first:last, :], q_ref[first:, :])
        mixing = jnp.where(keep, mixing, 0.0).astype(BF16)
        vp_ref[first:last, :] = mm(mixing, grad_ref[first:, :])


def inner(q, k, v, grad, state):
    tokens, width = q.shape
    spec = head_spec(tokens)
    return pl.pallas_call(
        functools.partial(inner_kernel, block_of(tokens, 256)),
        out_shape=(
            jax.ShapeDtypeStruct(q.shape, BF16),
            jax.ShapeDtypeStruct(q.shape, F32),
            jax.ShapeDtypeStruct(q.shape, F32),
        ),
        grid=(width // HEAD_DIM,),
        in_specs=[spec] * 4 + [SQUARE],
        out_specs=(spec, spec, spec),
        cost_estimate=cost(8 * tokens * tokens * width, 18 * tokens * width),
        name="inner",
    )(q, k, v, grad, state)


def finish_kernel(k_ref, v_ref, kp_ref, vp_ref, later_ref, kg_ref, vg_ref):
    later = later_ref[0].astype(BF16)
    kg_ref[...] = (kp_ref[...] + mmt(v_ref[...], later)).astype(BF16)
    vg_ref[...] = (vp_ref[...] + mm(k_ref[...], later)).astype(BF16)


def finish(k, v, kp, vp, later):
    tokens, width = k.shape
    spec = head_spec(tokens)
    return pl.pallas_call(
        finish_kernel,
        out_shape=(jax.ShapeDtypeStruct(k.shape, BF16),) * 2,
        grid=(width // HEAD_DIM,),
        in_specs=[spec] * 4 + [SQUARE],
        out_specs=(spec, spec),
        cost_estimate=cost(4 * tokens * width * HEAD_DIM, 16 * tokens * width),
        name="finish",
    )(k, v, kp, vp, later)


def per_device(n_seq, n_head, queries, keys, values, out_weight, cotangent):
    rows, columns = out_weight.shape[0], cotangent.shape[1]
    seq, head = lax.axis_index("seq"), lax.axis_index("head")
    where = jnp.stack([seq, head]).astype(jnp.int32)

    def toggled(x, mask):
        return lax.ppermute(x, "seq", [(i, i ^ mask) for i in range(n_seq)])

    share = rows // n_seq
    direct = n_seq <= 8
    order = tuple(range(n_seq)) if direct else (0,)
    pieces = {}
    near_first = [r for t in range(1, n_head) for r in sorted({n_head - t, t})]
    for r in dict.fromkeys(near_first):
        target = lax.rem(head - r + n_head, n_head)
        mine = lax.dynamic_slice(out_weight, (seq * share, target * columns), (share, columns))
        mine = lax.ppermute(mine, "head", [(i, (i - r) % n_head) for i in range(n_head)])
        if direct:
            even = [mine] + [toggled(mine, m) for m in range(2, n_seq, 2)]
            odd = [toggled(x, 1) for x in even]
            pieces[r] = [x for pair in zip(even, odd) for x in pair]
        else:
            pieces[r] = [lax.all_gather(mine, "seq", axis=0, tiled=True)]

    def place_of(where):
        return where if direct else where * jnp.array([0, 1], jnp.int32)

    def running(local, wanted):
        total, kept = local, jnp.zeros_like(local)
        mask = 1
        while mask < n_seq:
            came = toggled(total.astype(BF16), mask).astype(F32)
            kept = kept + jnp.where((seq & mask > 0) == wanted, came, 0.0)
            total = total + came
            mask *= 2
        return kept

    state = running(outer(keys, values), True)
    head_out, normed = forward(queries, keys, values, state)

    from_below, from_above = {}, {}
    below = above = normed
    for t in range(1, n_head):
        below = lax.ppermute(below, "head", [(i, i + 1) for i in range(t - 1, n_head - 1)])
        above = lax.ppermute(above, "head", [(i, i - 1) for i in range(1, n_head - t + 1)])
        from_below[t], from_above[t] = below, above

    near = own_partial(where, cotangent, out_weight)
    parts = {
        r: partial(place_of(where), cotangent, pieces[r], order, rows) for r in range(1, n_head)
    }
    up = down = None
    for t in range(1, n_head):
        up_part, down_part = parts[n_head - t], parts[t]
        if t > 1:
            up_part = (up_part.astype(F32) + up.astype(F32)).astype(BF16)
            down_part = (down_part.astype(F32) + down.astype(F32)).astype(BF16)
        up = lax.ppermute(up_part, "head", [(i, i + 1) for i in range(t)])
        down = lax.ppermute(
            down_part, "head", [(n_head - 1 - i, n_head - 2 - i) for i in range(t)]
        )

    mixed = mix(
        place_of(where),
        normed,
        out_weight,
        [([from_above[r], from_below[n_head - r]], pieces[r]) for r in range(1, n_head)],
        order,
        columns,
    )

    grad, local = grad_heads(near, up, down, head_out, queries)
    later = running(local, False)
    query_grad, key_part, value_part = inner(queries, keys, values, grad, state)
    key_grad, value_grad = finish(keys, values, key_part, value_part, later)
    return mixed, query_grad, key_grad, value_grad


def solution(mesh):
    placed = (
        P("seq", "head"),
        P("seq", "head"),
        P("seq", "head"),
        P("head", None),
        P("seq", "head"),
    )
    return jax.shard_map(
        functools.partial(per_device, mesh.shape["seq"], mesh.shape["head"]),
        mesh=mesh,
        in_specs=placed,
        out_specs=(P("seq", "head"),) * 4,
        check_vma=False,
    )
```

```python
import functools

import jax
import jax.numpy as jnp
from jax import lax
from jax.experimental import pallas as pl
from jax.experimental.pallas import tpu as pltpu
from jax.sharding import PartitionSpec as P

HEAD_DIM = 128
EPSILON = 1e-06
F32 = jnp.float32
BF16 = jnp.bfloat16


def dot(a, b, dims):
    return lax.dot_general(a, b, ((dims[:1], dims[1:]), ((), ())), preferred_element_type=F32)


def mm(a, b):
    return dot(a, b, (1, 0))


def mmt(a, b):
    return dot(a, b, (1, 1))


def tmm(a, b):
    return dot(a, b, (0, 0))


def block_of(extent, most):
    for size in (most, most // 2, most // 4):
        if extent % size == 0:
            return size
    return extent


def head_spec(tokens):
    return pl.BlockSpec((tokens, HEAD_DIM), lambda h: (0, h))


SQUARE = pl.BlockSpec((1, HEAD_DIM, HEAD_DIM), lambda h: (h, 0, 0))


def cost(flops, nbytes):
    return pl.CostEstimate(flops=int(flops), bytes_accessed=int(nbytes), transcendentals=0)


def later_key(rows, cols, base):
    at = lax.broadcasted_iota(jnp.int32, (rows, cols), 0) + base
    return at >= lax.broadcasted_iota(jnp.int32, (rows, cols), 1)


def later_query(rows, cols):
    at = lax.broadcasted_iota(jnp.int32, (rows, cols), 0)
    return lax.broadcasted_iota(jnp.int32, (rows, cols), 1) >= at


def outer_kernel(a_ref, b_ref, out_ref):
    out_ref[0] = tmm(a_ref[...], b_ref[...])


def outer(a, b):
    tokens, width = a.shape
    heads = width // HEAD_DIM
    return pl.pallas_call(
        outer_kernel,
        out_shape=jax.ShapeDtypeStruct((heads, HEAD_DIM, HEAD_DIM), F32),
        grid=(heads,),
        in_specs=[head_spec(tokens)] * 2,
        out_specs=SQUARE,
        cost_estimate=cost(2 * tokens * width * HEAD_DIM, 4 * tokens * width),
        name="outer",
    )(a, b)


def forward_kernel(step, q_ref, k_ref, v_ref, state_ref, out_ref, normed_ref):
    tokens = q_ref.shape[0]
    state = state_ref[0].astype(BF16)
    for first in range(0, tokens, step):
        last = first + step
        q = q_ref[first:last, :]
        mixing = mmt(q, k_ref[:last, :])
        mixing = jnp.where(later_key(step, last, first), mixing, 0.0).astype(BF16)
        out = mm(mixing, v_ref[:last, :]) + mm(q, state)
        inverse = lax.rsqrt(jnp.mean(out * out, axis=-1, keepdims=True) + EPSILON)
        out_ref[first:last, :] = out
        normed_ref[first:last, :] = (out * inverse).astype(BF16)


def forward(q, k, v, state):
    tokens, width = q.shape
    spec = head_spec(tokens)
    return pl.pallas_call(
        functools.partial(forward_kernel, block_of(tokens, 256)),
        out_shape=(jax.ShapeDtypeStruct(q.shape, F32), jax.ShapeDtypeStruct(q.shape, BF16)),
        grid=(width // HEAD_DIM,),
        in_specs=[spec] * 3 + [SQUARE],
        out_specs=(spec, spec),
        cost_estimate=cost(4 * tokens * tokens * width, 12 * tokens * width),
        name="forward",
    )(q, k, v, state)


def place(piece_refs, orders, seq, share, weight_ref):
    for ref, order in zip(piece_refs, orders):
        for at, mask in enumerate(order):
            start = pl.multiple_of((seq ^ mask) * share, share)
            weight_ref[pl.ds(start, share), :] = ref[at * share : (at + 1) * share, :]


def partial_kernel(orders, share, where_ref, cot_ref, *refs):
    pieces, (out_ref, weight_ref) = refs[: len(orders)], refs[len(orders) :]

    @pl.when(pl.program_id(0) == 0)
    def _():
        place(pieces, orders, where_ref[0], share, weight_ref)

    out_ref[...] = mmt(cot_ref[...], weight_ref[...]).astype(out_ref.dtype)


def partial(where, cot, pieces, orders, share):
    tokens, depth = cot.shape
    rows = sum(p.shape[0] for p in pieces)
    step = block_of(tokens, 256)
    return pl.pallas_call(
        functools.partial(partial_kernel, orders, share),
        out_shape=jax.ShapeDtypeStruct((tokens, rows), BF16),
        grid_spec=pltpu.PrefetchScalarGridSpec(
            num_scalar_prefetch=1,
            grid=(tokens // step,),
            in_specs=[pl.BlockSpec((step, depth), lambda i, w: (i, 0))]
            + [pl.BlockSpec(p.shape, lambda i, w: (0, 0)) for p in pieces],
            out_specs=pl.BlockSpec((step, rows), lambda i, w: (i, 0)),
            scratch_shapes=[pltpu.VMEM((rows, depth), BF16)],
        ),
        cost_estimate=cost(2 * tokens * depth * rows, 2 * (tokens + rows) * depth),
        name="partial",
    )(where, cot, *pieces)


def own_partial_kernel(where_ref, cot_ref, weight_ref, out_ref):
    out_ref[...] = mmt(cot_ref[...], weight_ref[...])


def own_partial(where, cot, weight):
    tokens, depth = cot.shape
    rows = weight.shape[0]
    step = block_of(tokens, 256)
    return pl.pallas_call(
        own_partial_kernel,
        out_shape=jax.ShapeDtypeStruct((tokens, rows), F32),
        grid_spec=pltpu.PrefetchScalarGridSpec(
            num_scalar_prefetch=1,
            grid=(tokens // step,),
            in_specs=[
                pl.BlockSpec((step, depth), lambda i, w: (i, 0)),
                pl.BlockSpec((rows, depth), lambda i, w: (0, w[1])),
            ],
            out_specs=pl.BlockSpec((step, rows), lambda i, w: (i, 0)),
        ),
        cost_estimate=cost(2 * tokens * depth * rows, 2 * (tokens + rows) * depth),
        name="own_partial",
    )(where, cot, weight)


def mixed_kernel(sources, orders, share, where_ref, own_ref, weight_ref, *refs):
    normed_refs, refs = refs[: len(sources[0][1])], refs[len(sources[0][1]) :]
    out_ref, scratch_ref, chosen_ref = refs[-3:]

    @pl.when(pl.program_id(0) == 0)
    def _():
        for at, (_, picks) in enumerate(sources):
            for ref, heads in zip(normed_refs, picks):
                for head in heads:

                    @pl.when(where_ref[1] == head)
                    def _():
                        chosen_ref[at] = ref[...]

    total = mm(own_ref[...], weight_ref[...])
    per = len(orders)
    for at in range(len(sources)):
        place(refs[at * per : (at + 1) * per], orders, where_ref[0], share, scratch_ref)
        total += mm(chosen_ref[at], scratch_ref[...])
    out_ref[...] = total.astype(BF16)


def mix(where, own, weight, came, sources, pieces, orders, share, columns):
    tokens, rows = own.shape
    step = block_of(columns, 512)
    count = columns // step
    full = pl.BlockSpec((tokens, rows), lambda i, w: (0, 0))
    specs = [full, pl.BlockSpec((rows, step), lambda i, w: (0, w[1] * count + i))]
    specs += [full] * len(came)
    operands = [own, weight, *came]
    for m, _ in sources:
        specs += [pl.BlockSpec((p.shape[0], step), lambda i, w: (0, i)) for p in pieces[m]]
        operands += pieces[m]
    n = len(sources) + 1
    return pl.pallas_call(
        functools.partial(mixed_kernel, sources, orders, share),
        out_shape=jax.ShapeDtypeStruct((tokens, columns), BF16),
        grid_spec=pltpu.PrefetchScalarGridSpec(
            num_scalar_prefetch=1,
            grid=(count,),
            in_specs=specs,
            out_specs=pl.BlockSpec((tokens, step), lambda i, w: (0, i)),
            scratch_shapes=[
                pltpu.VMEM((rows, step), BF16),
                pltpu.VMEM((n - 1, tokens, rows), BF16),
            ],
        ),
        cost_estimate=cost(2 * tokens * rows * n * columns, 2 * n * rows * (tokens + columns)),
        name="mix",
    )(where, *operands)


def grad_heads_kernel(own_ref, up_ref, down_ref, out_ref, q_ref, grad_ref, local_ref):
    grad = own_ref[...] + up_ref[...].astype(F32) + down_ref[...].astype(F32)
    out = out_ref[...]
    inverse = lax.rsqrt(jnp.mean(out * out, axis=-1, keepdims=True) + EPSILON)
    normed = out * inverse
    aligned = jnp.mean(grad * normed, axis=-1, keepdims=True)
    grad = (inverse * (grad - normed * aligned)).astype(BF16)
    grad_ref[...] = grad
    local_ref[0] = tmm(q_ref[...], grad)


def grad_heads(own, up, down, out, q):
    tokens, width = q.shape
    heads = width // HEAD_DIM
    spec = head_spec(tokens)
    return pl.pallas_call(
        grad_heads_kernel,
        out_shape=(
            jax.ShapeDtypeStruct(q.shape, BF16),
            jax.ShapeDtypeStruct((heads, HEAD_DIM, HEAD_DIM), F32),
        ),
        grid=(heads,),
        in_specs=[spec] * 5,
        out_specs=(spec, SQUARE),
        cost_estimate=cost(2 * tokens * width * HEAD_DIM, 16 * tokens * width),
        name="grad_heads",
    )(own, up, down, out, q)


def inner_kernel(step, q_ref, k_ref, v_ref, grad_ref, state_ref, qg_ref, kp_ref, vp_ref):
    tokens = q_ref.shape[0]
    state = state_ref[0].astype(BF16)
    for first in range(0, tokens, step):
        last = first + step
        grad = grad_ref[first:last, :]
        cross = mmt(grad, v_ref[:last, :])
        cross = jnp.where(later_key(step, last, first), cross, 0.0).astype(BF16)
        qg_ref[first:last, :] = (mm(cross, k_ref[:last, :]) + mmt(grad, state)).astype(BF16)
        keep = later_query(step, tokens - first)
        cross = mmt(v_ref[first:last, :], grad_ref[first:, :])
        cross = jnp.where(keep, cross, 0.0).astype(BF16)
        kp_ref[first:last, :] = mm(cross, q_ref[first:, :])
        mixing = mmt(k_ref[first:last, :], q_ref[first:, :])
        mixing = jnp.where(keep, mixing, 0.0).astype(BF16)
        vp_ref[first:last, :] = mm(mixing, grad_ref[first:, :])


def inner(q, k, v, grad, state):
    tokens, width = q.shape
    spec = head_spec(tokens)
    return pl.pallas_call(
        functools.partial(inner_kernel, block_of(tokens, 256)),
        out_shape=(
            jax.ShapeDtypeStruct(q.shape, BF16),
            jax.ShapeDtypeStruct(q.shape, F32),
            jax.ShapeDtypeStruct(q.shape, F32),
        ),
        grid=(width // HEAD_DIM,),
        in_specs=[spec] * 4 + [SQUARE],
        out_specs=(spec, spec, spec),
        cost_estimate=cost(8 * tokens * tokens * width, 18 * tokens * width),
        name="inner",
    )(q, k, v, grad, state)


def finish_kernel(k_ref, v_ref, kp_ref, vp_ref, later_ref, kg_ref, vg_ref):
    later = later_ref[0].astype(BF16)
    kg_ref[...] = (kp_ref[...] + mmt(v_ref[...], later)).astype(BF16)
    vg_ref[...] = (vp_ref[...] + mm(k_ref[...], later)).astype(BF16)


def finish(k, v, kp, vp, later):
    tokens, width = k.shape
    spec = head_spec(tokens)
    return pl.pallas_call(
        finish_kernel,
        out_shape=(jax.ShapeDtypeStruct(k.shape, BF16),) * 2,
        grid=(width // HEAD_DIM,),
        in_specs=[spec] * 4 + [SQUARE],
        out_specs=(spec, spec),
        cost_estimate=cost(4 * tokens * width * HEAD_DIM, 16 * tokens * width),
        name="finish",
    )(k, v, kp, vp, later)


def per_device(n_seq, n_head, queries, keys, values, out_weight, cotangent):
    rows, columns = out_weight.shape[0], cotangent.shape[1]
    seq, head = lax.axis_index("seq"), lax.axis_index("head")
    where = jnp.stack([seq, head]).astype(jnp.int32)

    def toggled(x, mask):
        return lax.ppermute(x, "seq", [(i, i ^ mask) for i in range(n_seq)])

    share = rows // n_seq
    direct = n_seq <= 8
    if direct:
        orders = (tuple(range(0, n_seq, 2)), tuple(range(1, n_seq, 2)))
    else:
        orders, share, where_rows = ((0,),), rows, where * jnp.array([0, 1], jnp.int32)
    pieces = {}
    masks = range(n_head - 1, 0, -1)
    for m in masks:
        cut = rows // n_seq
        mine = lax.dynamic_slice(out_weight, (seq * cut, (head ^ m) * columns), (cut, columns))
        mine = lax.ppermute(mine, "head", [(i, i ^ m) for i in range(n_head)])
        if direct:
            even = [mine] + [toggled(mine, k) for k in range(2, n_seq, 2)]
            even = jnp.concatenate(even, axis=0)
            pieces[m] = [even, toggled(even, 1)]
        else:
            pieces[m] = [lax.all_gather(mine, "seq", axis=0, tiled=True)]
    if direct:
        where_rows = where

    def running(local, wanted):
        total, kept = local, jnp.zeros_like(local)
        mask = 1
        while mask < n_seq:
            came = toggled(total.astype(BF16), mask).astype(F32)
            kept = kept + jnp.where((seq & mask > 0) == wanted, came, 0.0)
            total = total + came
            mask *= 2
        return kept

    state = running(outer(keys, values), True)
    head_out, normed = forward(queries, keys, values, state)
    near = own_partial(where, cotangent, out_weight)
    parts = {m: partial(where_rows, cotangent, pieces[m], orders, share) for m in masks}

    def step_out(t, place_in_line, target, came):
        if t == 0:
            return normed
        chosen = None
        for i in range(t):
            part = parts[i ^ (i + n_head - t)]
            chosen = part if chosen is None else jnp.where(place_in_line == i, part, chosen)
        chosen = jnp.where(place_in_line < t, chosen.astype(F32), 0.0)
        return (came.astype(F32) + chosen).astype(BF16)

    up = down = None
    ups, downs = [], []
    for t in range(n_head):
        up = lax.ppermute(
            step_out(t, head, t, up), "head", [(i, i + 1) for i in range(n_head - 1)]
        )
        down = lax.ppermute(
            step_out(t, n_head - 1 - head, t, down),
            "head",
            [(i + 1, i) for i in range(n_head - 1)],
        )
        ups.append(up)
        downs.append(down)

    sources = []
    for m in masks:
        picks = [[i for i in range(n_head) if i - (i ^ m) == t + 1] for t in range(n_head - 1)]
        picks += [[i for i in range(n_head) if (i ^ m) - i == t + 1] for t in range(n_head - 1)]
        sources.append((m, picks))
    mixed = mix(
        where_rows,
        normed,
        out_weight,
        ups[:-1] + downs[:-1],
        sources,
        pieces,
        orders,
        share,
        columns,
    )
    up, down, mixed = lax.optimization_barrier((up, down, mixed))

    grad, local = grad_heads(near, up, down, head_out, queries)
    later = running(local, False)
    query_grad, key_part, value_part = inner(queries, keys, values, grad, state)
    key_grad, value_grad = finish(keys, values, key_part, value_part, later)
    return mixed, query_grad, key_grad, value_grad


def solution(mesh):
    placed = (
        P("seq", "head"),
        P("seq", "head"),
        P("seq", "head"),
        P("head", None),
        P("seq", "head"),
    )
    return jax.shard_map(
        functools.partial(per_device, mesh.shape["seq"], mesh.shape["head"]),
        mesh=mesh,
        in_specs=placed,
        out_specs=(P("seq", "head"),) * 4,
        check_vma=False,
    )
```

```python
import functools

import jax
import jax.numpy as jnp
from jax import lax
from jax.experimental import pallas as pl
from jax.experimental.pallas import tpu as pltpu
from jax.sharding import PartitionSpec as P

HEAD_DIM = 128
EPSILON = 1e-06
F32 = jnp.float32
BF16 = jnp.bfloat16


def dot(a, b, dims):
    return lax.dot_general(a, b, ((dims[:1], dims[1:]), ((), ())), preferred_element_type=F32)


def mm(a, b):
    return dot(a, b, (1, 0))


def mmt(a, b):
    return dot(a, b, (1, 1))


def tmm(a, b):
    return dot(a, b, (0, 0))


def block_of(extent, most):
    for size in (most, most // 2, most // 4):
        if extent % size == 0:
            return size
    return extent


def head_spec(tokens, first=0):
    return pl.BlockSpec((tokens, HEAD_DIM), lambda h: (0, h + first))


def square_spec(first):
    return pl.BlockSpec((1, HEAD_DIM, HEAD_DIM), lambda h: (h + first, 0, 0))


SQUARE = square_spec(0)


def cost(flops, nbytes):
    return pl.CostEstimate(flops=int(flops), bytes_accessed=int(nbytes), transcendentals=0)


def later_key(rows, cols, base):
    at = lax.broadcasted_iota(jnp.int32, (rows, cols), 0) + base
    return at >= lax.broadcasted_iota(jnp.int32, (rows, cols), 1)


def later_query(rows, cols):
    at = lax.broadcasted_iota(jnp.int32, (rows, cols), 0)
    return lax.broadcasted_iota(jnp.int32, (rows, cols), 1) >= at


def outer_kernel(a_ref, b_ref, out_ref, sent_ref):
    state = tmm(a_ref[...], b_ref[...])
    out_ref[0] = state
    sent_ref[0] = state.astype(BF16)


def outer(a, b):
    tokens, width = a.shape
    heads = width // HEAD_DIM
    shape = (heads, HEAD_DIM, HEAD_DIM)
    return pl.pallas_call(
        outer_kernel,
        out_shape=(jax.ShapeDtypeStruct(shape, F32), jax.ShapeDtypeStruct(shape, BF16)),
        grid=(heads,),
        in_specs=[head_spec(tokens)] * 2,
        out_specs=(SQUARE, SQUARE),
        cost_estimate=cost(2 * tokens * width * HEAD_DIM, 4 * tokens * width),
        name="outer",
    )(a, b)


def forward_kernel(step, q_ref, k_ref, v_ref, state_ref, out_ref, normed_ref):
    tokens = q_ref.shape[0]
    state = state_ref[0].astype(BF16)
    for first in range(0, tokens, step):
        last = first + step
        q = q_ref[first:last, :]
        mixing = mmt(q, k_ref[:last, :])
        mixing = jnp.where(later_key(step, last, first), mixing, 0.0).astype(BF16)
        out = mm(mixing, v_ref[:last, :]) + mm(q, state)
        inverse = lax.rsqrt(jnp.mean(out * out, axis=-1, keepdims=True) + EPSILON)
        out_ref[first:last, :] = out
        normed_ref[first:last, :] = (out * inverse).astype(BF16)


def forward(q, k, v, state, first, heads):
    tokens = q.shape[0]
    width = heads * HEAD_DIM
    spec = head_spec(tokens, first)
    return pl.pallas_call(
        functools.partial(forward_kernel, block_of(tokens, 256)),
        out_shape=(
            jax.ShapeDtypeStruct((tokens, width), F32),
            jax.ShapeDtypeStruct((tokens, width), BF16),
        ),
        grid=(heads,),
        in_specs=[spec] * 3 + [square_spec(first)],
        out_specs=(head_spec(tokens), head_spec(tokens)),
        cost_estimate=cost(4 * tokens * tokens * width, 12 * tokens * width),
        name="forward",
    )(q, k, v, state)


def place(piece_refs, orders, seq, share, weight_ref):
    for ref, order in zip(piece_refs, orders):
        for at, mask in enumerate(order):
            start = pl.multiple_of((seq ^ mask) * share, share)
            weight_ref[pl.ds(start, share), :] = ref[at * share : (at + 1) * share, :]


def partial_kernel(orders, share, where_ref, cot_ref, *refs):
    pieces, outs, weight_ref = refs[: len(orders)], refs[len(orders) : -1], refs[-1]

    @pl.when(pl.program_id(0) == 0)
    def _():
        place(pieces, orders, where_ref[0], share, weight_ref)

    part = mmt(cot_ref[...], weight_ref[...]).astype(BF16)
    width = part.shape[1] // len(outs)
    for at, out_ref in enumerate(outs):
        out_ref[...] = part[:, at * width : (at + 1) * width]


def partial(where, cot, pieces, orders, share, splits):
    tokens, depth = cot.shape
    rows = sum(p.shape[0] for p in pieces)
    step = block_of(tokens, 256)
    return pl.pallas_call(
        functools.partial(partial_kernel, orders, share),
        out_shape=(jax.ShapeDtypeStruct((tokens, rows // splits), BF16),) * splits,
        grid_spec=pltpu.PrefetchScalarGridSpec(
            num_scalar_prefetch=1,
            grid=(tokens // step,),
            in_specs=[pl.BlockSpec((step, depth), lambda i, w: (i, 0))]
            + [pl.BlockSpec(p.shape, lambda i, w: (0, 0)) for p in pieces],
            out_specs=(pl.BlockSpec((step, rows // splits), lambda i, w: (i, 0)),) * splits,
            scratch_shapes=[pltpu.VMEM((rows, depth), BF16)],
        ),
        cost_estimate=cost(2 * tokens * depth * rows, 2 * (tokens + rows) * depth),
        name="partial",
    )(where, cot, *pieces)


def own_partial_kernel(where_ref, cot_ref, weight_ref, out_ref):
    out_ref[...] = mmt(cot_ref[...], weight_ref[...])


def own_partial(where, cot, weight):
    tokens, depth = cot.shape
    rows = weight.shape[0]
    step = block_of(tokens, 256)
    return pl.pallas_call(
        own_partial_kernel,
        out_shape=jax.ShapeDtypeStruct((tokens, rows), F32),
        grid_spec=pltpu.PrefetchScalarGridSpec(
            num_scalar_prefetch=1,
            grid=(tokens // step,),
            in_specs=[
                pl.BlockSpec((step, depth), lambda i, w: (i, 0)),
                pl.BlockSpec((rows, depth), lambda i, w: (0, w[1])),
            ],
            out_specs=pl.BlockSpec((step, rows), lambda i, w: (i, 0)),
        ),
        cost_estimate=cost(2 * tokens * depth * rows, 2 * (tokens + rows) * depth),
        name="own_partial",
    )(where, cot, weight)


def mixed_kernel(sources, orders, share, splits, where_ref, *refs):
    refs = list(refs)
    own_refs = [refs.pop(0) for _ in range(splits)]
    weight_ref = refs.pop(0)
    normed_refs = [refs.pop(0) for _ in range(splits * len(sources[0][1]))]
    out_ref, scratch_ref, chosen_ref = refs[-3:]
    width = own_refs[0].shape[1]

    @pl.when(pl.program_id(0) == 0)
    def _():
        for part in range(splits):
            columns = slice(part * width, (part + 1) * width)
            chosen_ref[0, :, columns] = own_refs[part][...]
            for at, (_, picks) in enumerate(sources):
                for ref, heads in zip(normed_refs[part::splits], picks):
                    for head in heads:

                        @pl.when(where_ref[1] == head)
                        def _():
                            chosen_ref[at + 1, :, columns] = ref[...]

    total = mm(chosen_ref[0], weight_ref[...])
    per = len(orders)
    for at in range(len(sources)):
        place(refs[at * per : (at + 1) * per], orders, where_ref[0], share, scratch_ref)
        total += mm(chosen_ref[at + 1], scratch_ref[...])
    out_ref[...] = total.astype(BF16)


def mix(where, own, weight, came, sources, pieces, orders, share, columns):
    splits = len(own)
    tokens, rows = own[0].shape[0], weight.shape[0]
    step = block_of(columns, 512)
    count = columns // step
    full = pl.BlockSpec(own[0].shape, lambda i, w: (0, 0))
    specs = [full] * splits + [pl.BlockSpec((rows, step), lambda i, w: (0, w[1] * count + i))]
    specs += [full] * (splits * len(came))
    operands = [*own, weight] + [x for pair in came for x in pair]
    for m, _ in sources:
        specs += [pl.BlockSpec((p.shape[0], step), lambda i, w: (0, i)) for p in pieces[m]]
        operands += pieces[m]
    n = len(sources) + 1
    return pl.pallas_call(
        functools.partial(mixed_kernel, sources, orders, share, splits),
        out_shape=jax.ShapeDtypeStruct((tokens, columns), BF16),
        grid_spec=pltpu.PrefetchScalarGridSpec(
            num_scalar_prefetch=1,
            grid=(count,),
            in_specs=specs,
            out_specs=pl.BlockSpec((tokens, step), lambda i, w: (0, i)),
            scratch_shapes=[
                pltpu.VMEM((rows, step), BF16),
                pltpu.VMEM((n, tokens, rows), BF16),
            ],
        ),
        cost_estimate=cost(2 * tokens * rows * n * columns, 2 * n * rows * (tokens + columns)),
        name="mix",
    )(where, *operands)


def extend(kernel, operands, specs, earlier):
    if earlier is None:
        return kernel, operands, specs, {}
    count = len(operands)
    aliases = {count + at: at for at in range(len(earlier))}
    return (
        lambda *refs: kernel(*refs[:count], *refs[count + len(earlier) :]),
        [*operands, *earlier],
        [*specs] + [pl.BlockSpec(memory_space=pl.ANY)] * len(earlier),
        aliases,
    )


def grad_heads_kernel(own_ref, up_ref, down_ref, out_ref, q_ref, grad_ref, local_ref, sent_ref):
    grad = own_ref[...] + up_ref[...].astype(F32) + down_ref[...].astype(F32)
    out = out_ref[...]
    inverse = lax.rsqrt(jnp.mean(out * out, axis=-1, keepdims=True) + EPSILON)
    normed = out * inverse
    aligned = jnp.mean(grad * normed, axis=-1, keepdims=True)
    grad = (inverse * (grad - normed * aligned)).astype(BF16)
    grad_ref[...] = grad
    local = tmm(q_ref[...], grad)
    local_ref[0] = local
    sent_ref[0] = local.astype(BF16)


def grad_heads(own, up, down, out, q, first, heads):
    tokens = q.shape[0]
    width = heads * HEAD_DIM
    spec, whole = head_spec(tokens), head_spec(tokens, first)
    shape = (heads, HEAD_DIM, HEAD_DIM)
    return pl.pallas_call(
        grad_heads_kernel,
        out_shape=(
            jax.ShapeDtypeStruct((tokens, width), BF16),
            jax.ShapeDtypeStruct(shape, F32),
            jax.ShapeDtypeStruct(shape, BF16),
        ),
        grid=(heads,),
        in_specs=[whole, spec, spec, spec, whole],
        out_specs=(spec, SQUARE, SQUARE),
        cost_estimate=cost(2 * tokens * width * HEAD_DIM, 16 * tokens * width),
        name="grad_heads",
    )(own, up, down, out, q)


def inner_kernel(step, q_ref, k_ref, v_ref, grad_ref, state_ref, qg_ref, kp_ref, vp_ref):
    tokens = q_ref.shape[0]
    state = state_ref[0].astype(BF16)
    for first in range(0, tokens, step):
        last = first + step
        grad = grad_ref[first:last, :]
        cross = mmt(grad, v_ref[:last, :])
        cross = jnp.where(later_key(step, last, first), cross, 0.0).astype(BF16)
        qg_ref[first:last, :] = (mm(cross, k_ref[:last, :]) + mmt(grad, state)).astype(BF16)
        keep = later_query(step, tokens - first)
        cross = mmt(v_ref[first:last, :], grad_ref[first:, :])
        cross = jnp.where(keep, cross, 0.0).astype(BF16)
        kp_ref[first:last, :] = mm(cross, q_ref[first:, :])
        mixing = mmt(k_ref[first:last, :], q_ref[first:, :])
        mixing = jnp.where(keep, mixing, 0.0).astype(BF16)
        vp_ref[first:last, :] = mm(mixing, grad_ref[first:, :])


def inner(q, k, v, grad, state, first, heads, earlier):
    tokens = q.shape[0]
    width = heads * HEAD_DIM
    spec, whole = head_spec(tokens), head_spec(tokens, first)
    part = jax.ShapeDtypeStruct((tokens, width), F32)
    kernel, operands, specs, aliases = extend(
        functools.partial(inner_kernel, block_of(tokens, 256)),
        [q, k, v, grad, state],
        [whole, whole, whole, spec, square_spec(first)],
        earlier,
    )
    return pl.pallas_call(
        kernel,
        out_shape=(jax.ShapeDtypeStruct(q.shape, BF16), part, part),
        grid=(heads,),
        in_specs=specs,
        out_specs=(whole, spec, spec),
        input_output_aliases=aliases,
        cost_estimate=cost(8 * tokens * tokens * width, 18 * tokens * width),
        name="inner",
    )(*operands)


def finish_kernel(k_ref, v_ref, kp_ref, vp_ref, later_ref, kg_ref, vg_ref):
    later = later_ref[0].astype(BF16)
    kg_ref[...] = (kp_ref[...] + mmt(v_ref[...], later)).astype(BF16)
    vg_ref[...] = (vp_ref[...] + mm(k_ref[...], later)).astype(BF16)


def finish(k, v, kp, vp, later, first, heads, earlier):
    tokens = k.shape[0]
    width = heads * HEAD_DIM
    spec, whole = head_spec(tokens), head_spec(tokens, first)
    kernel, operands, specs, aliases = extend(
        finish_kernel,
        [k, v, kp, vp, later],
        [whole, whole, spec, spec, SQUARE],
        earlier,
    )
    return pl.pallas_call(
        kernel,
        out_shape=(jax.ShapeDtypeStruct(k.shape, BF16),) * 2,
        grid=(heads,),
        in_specs=specs,
        out_specs=(whole, whole),
        input_output_aliases=aliases,
        cost_estimate=cost(4 * tokens * width * HEAD_DIM, 16 * tokens * width),
        name="finish",
    )(*operands)


def per_device(n_seq, n_head, queries, keys, values, out_weight, cotangent):
    rows, columns = out_weight.shape[0], cotangent.shape[1]
    all_heads = rows // HEAD_DIM
    splits = 2 if all_heads % 2 == 0 else 1
    heads = all_heads // splits
    seq, head = lax.axis_index("seq"), lax.axis_index("head")
    where = jnp.stack([seq, head]).astype(jnp.int32)
    direct = n_seq <= 8

    def toggled(x, mask):
        return lax.ppermute(x, "seq", [(i, i ^ mask) for i in range(n_seq)])

    def others(local, sent, before):
        def wanted(mask):
            return ((seq ^ mask) < seq) == before

        came = toggled(sent, 1).astype(F32)
        total, kept = local + came, jnp.where(wanted(1), came, 0.0)
        if direct:
            sent = total.astype(BF16)
            for mask in range(2, n_seq, 2):
                kept += jnp.where(wanted(mask), toggled(sent, mask).astype(F32), 0.0)
            return kept
        mask = 2
        while mask < n_seq:
            came = toggled(total.astype(BF16), mask).astype(F32)
            kept += jnp.where(wanted(mask), came, 0.0)
            total += came
            mask *= 2
        return kept

    share = rows // n_seq
    masks = range(n_head - 1, 0, -1)
    mine = {}
    for m in masks:
        cut = lax.dynamic_slice(
            out_weight, (seq * share, (head ^ m) * columns), (share, columns)
        )
        mine[m] = lax.ppermute(cut, "head", [(i, i ^ m) for i in range(n_head)])

    state = others(*outer(keys, values), True)

    pieces, last = {}, state
    for m in masks:
        if direct:
            own, last = lax.optimization_barrier((mine[m], last))
            if m == masks[0]:
                state = last
            even = [own] + [toggled(own, k) for k in range(2, n_seq, 2)]
            even = last = jnp.concatenate(even, axis=0)
            pieces[m] = [even, toggled(even, 1)]
        else:
            pieces[m] = [lax.all_gather(mine[m], "seq", axis=0, tiled=True)]
    if direct:
        orders, where_rows = (tuple(range(0, n_seq, 2)), tuple(range(1, n_seq, 2))), where
    else:
        orders, share, where_rows = ((0,),), rows, where * jnp.array([0, 1], jnp.int32)

    head_out, normed = zip(
        *[
            forward(queries, keys, values, state, part * heads, heads)
            for part in range(splits)
        ]
    )
    near = own_partial(where, cotangent, out_weight)
    parts = {
        m: partial(where_rows, cotangent, pieces[m], orders, share, splits) for m in masks
    }

    def step_out(t, part, place_in_line, came):
        if t == 0:
            return normed[part]
        chosen = None
        for i in range(t):
            term = parts[i ^ (i + n_head - t)][part]
            chosen = term if chosen is None else jnp.where(place_in_line == i, term, chosen)
        chosen = jnp.where(place_in_line < t, chosen.astype(F32), 0.0)
        return (came.astype(F32) + chosen).astype(BF16)

    up, down = [None] * splits, [None] * splits
    ups, downs = [], []
    for t in range(n_head):
        for part in range(splits):
            up[part] = lax.ppermute(
                step_out(t, part, head, up[part]),
                "head",
                [(i, i + 1) for i in range(n_head - 1)],
            )
            down[part] = lax.ppermute(
                step_out(t, part, n_head - 1 - head, down[part]),
                "head",
                [(i + 1, i) for i in range(n_head - 1)],
            )
        ups.append(tuple(up))
        downs.append(tuple(down))

    sources = []
    for m in masks:
        picks = [[i for i in range(n_head) if i - (i ^ m) == t + 1] for t in range(n_head - 1)]
        picks += [[i for i in range(n_head) if (i ^ m) - i == t + 1] for t in range(n_head - 1)]
        sources.append((m, picks))
    mixed = mix(
        where_rows,
        normed,
        out_weight,
        ups[:-1] + downs[:-1],
        sources,
        pieces,
        orders,
        share,
        columns,
    )
    up[0], down[0], mixed = lax.optimization_barrier((up[0], down[0], mixed))

    query_grad, ends = None, None
    for part in range(splits):
        first = part * heads
        grad, local, sent = grad_heads(
            near, up[part], down[part], head_out[part], queries, first, heads
        )
        later = others(local, sent, False)
        query_grad, key_part, value_part = inner(
            queries,
            keys,
            values,
            grad,
            state,
            first,
            heads,
            None if query_grad is None else [query_grad],
        )
        ends = finish(keys, values, key_part, value_part, later, first, heads, ends)
    return (mixed, query_grad, *ends)


def solution(mesh):
    placed = (
        P("seq", "head"),
        P("seq", "head"),
        P("seq", "head"),
        P("head", None),
        P("seq", "head"),
    )
    return jax.shard_map(
        functools.partial(per_device, mesh.shape["seq"], mesh.shape["head"]),
        mesh=mesh,
        in_specs=placed,
        out_specs=(P("seq", "head"),) * 4,
        check_vma=False,
    )
```
